32 devices in a mesh: member: 2 (over core), shard: 16 (over z, y, x).
Axes of the slice: x: 2, y: 2, z: 4, core: 2. Of those that a mesh axis runs over, the one named last changes fastest.
Arguments:
- layer_input: bfloat16 [2, 180, 5120], P('member', None, 'shard'), may hold values from -6 to 6
- norm_gain: float32 [2, 5120], P('member'), may hold values from 0.5 to 2
- w_gate: bfloat16 [2, 5120, 1792], P('member', None, 'shard'), may hold values from -0.0559017 to 0.0559017
- w_up: bfloat16 [2, 5120, 1792], P('member', None, 'shard'), may hold values from -0.0559017 to 0.0559017
- hidden_cot: bfloat16 [2, 180, 1792], P('member', None, 'shard'), may hold values from -3 to 5
- output_cot: bfloat16 [2, 180, 5120], P('member', None, 'shard'), may hold values from -6 to 6
- embed: bfloat16 [2, 4096, 5120], P('member', 'shard'), may hold values from -0.078125 to 0.078125
- suffix_ids: int32 [180], replicated, may hold values from 0 to 4095
Outputs:
- delta: float32 [180, 4096], P(None, 'shard')
The draws below stay inside these ranges and needn't reach their ends.
All inputs are finite; a program needn't handle non-finite values.
Results may differ from the reference program's by a relative error of at most 0.0047.
Values may be sent and summed in bfloat16 or wider, within the bound.
A program may use at most 64 MiB of HBM per device.

```python
import math
import jax
import jax.numpy as jnp
from jax import lax

D = 5120
MEMBERS = 2
FFW = 1792
VOCAB = 4096
ROWS = 180


def weight_draw(key, own_tag):
    shape = (MEMBERS, D, FFW)
    common_part = jax.random.normal(jax.random.fold_in(key, 101), shape, jnp.float32)
    own_part = jax.random.normal(jax.random.fold_in(key, own_tag), shape, jnp.float32)
    mixed = 0.9 * common_part + 0.43588989 * own_part
    mixed = jnp.clip(mixed, -3.98, 3.98)
    return (mixed / jnp.sqrt(jnp.float32(D))).astype(jnp.bfloat16)


def draw_w_gate(key, part):
    return weight_draw(key, 102)


def draw_w_up(key, part):
    return weight_draw(key, 103)


def draw_hidden_cot(key, part):
    shape = (MEMBERS, ROWS, FFW)
    row_mean = jnp.ones((MEMBERS, ROWS, 1), jnp.float32)
    noise = jax.random.normal(jax.random.fold_in(key, 202), shape, jnp.float32)
    values = jnp.clip(row_mean + noise, -3.0, 5.0)
    return values.astype(jnp.bfloat16)


def place_ends(array, stream_key, least, top_value):
    longest = array.shape.index(max(array.shape))
    spots = []
    for shift in (0, 1):
        where = [jax.random.randint(jax.random.fold_in(stream_key, axis), (), 0, length) for axis, length in enumerate(array.shape)]
        where[longest] = (where[longest] + shift) % array.shape[longest]
        spots.append(tuple(where))
    return array.at[spots[0]].set(least).at[spots[1]].set(top_value)


def block_scale(own_key, extent, shards, least, largest):
    level, own = 1.0, jax.random.fold_in(own_key, 6)
    for dim, blocks in shards:
        draws = jnp.exp(jax.random.uniform(jax.random.fold_in(own, dim), (blocks,), jnp.float32, least / len(shards), largest / len(shards)))
        level = level * jnp.repeat(draws, extent[dim] // blocks).reshape([-1 if axis == dim else 1 for axis in range(len(extent))])
    return level


def scatter_about(key, dims, deviation, limit, shards=(), dtype=jnp.bfloat16):
    result = jax.random.normal(key, dims, jnp.float32) * deviation
    if len(shards) > 0:
        result = block_scale(key, dims, shards, -0.22, 0.18) * result
    return jnp.clip(result, min=-limit, max=limit).astype(dtype)


def setup_inputs(seed: int = 0) -> dict:
    key_list = jax.random.split(jax.random.key(seed), 9)
    return {
        "layer_input": scatter_about(key_list[0], (MEMBERS, ROWS, D), 1.0, 6.0, ((0, 2), (2, 16))),
        "norm_gain": jnp.clip(jnp.exp(math.log(2.0) - 1.3862944 * jax.random.uniform(key_list[1], (MEMBERS, D), jnp.float32) ** block_scale(key_list[1], (MEMBERS, D), ((0, 2),), -0.2, 0.2)), 0.5, 2.0),
        "w_gate": draw_w_gate(jax.random.fold_in(key_list[8], 71), 0),
        "w_up": draw_w_up(jax.random.fold_in(key_list[8], 71), 0),
        "hidden_cot": draw_hidden_cot(jax.random.fold_in(key_list[8], 71), 0),
        "output_cot": scatter_about(key_list[5], (MEMBERS, ROWS, D), 1.0, 6.0, ((0, 2), (2, 16))),
        "embed": scatter_about(key_list[6], (MEMBERS, VOCAB, D), D ** -0.5, 0.078125, ((0, 2), (1, 16))),
        "suffix_ids": place_ends(jax.random.randint(key_list[7], (ROWS,), 0, VOCAB), jax.random.fold_in(key_list[7], 1), 0, VOCAB - 1).astype(jnp.int32),
    }


def member_term(inputs_bf, gain, gate_w, up_w, hid_grad, out_grad, table, suffix_ids):
    inputs = inputs_bf.astype(jnp.float32)
    inv_rms = 1.0 / jnp.sqrt(lax.optimization_barrier(jnp.mean(inputs * inputs, axis=1, keepdims=True)) + 1e-05)
    normed = (inputs * inv_rms * gain[None, :]).astype(jnp.bfloat16)
    gate_pre = jnp.dot(normed, gate_w, preferred_element_type=jnp.float32)
    up_proj = jnp.dot(normed, up_w, preferred_element_type=jnp.float32)
    sigmoid_gate = jax.nn.sigmoid(gate_pre)
    hid_f = hid_grad.astype(jnp.float32)
    gate_grad = (hid_f * up_proj * sigmoid_gate * (1.0 + gate_pre * (1.0 - sigmoid_gate))).astype(jnp.bfloat16)
    up_grad = (hid_f * gate_pre * sigmoid_gate).astype(jnp.bfloat16)
    normed_grad = jnp.dot(gate_grad, gate_w.T, preferred_element_type=jnp.float32)
    normed_grad = normed_grad + jnp.dot(up_grad, up_w.T, preferred_element_type=jnp.float32)
    scaled = normed_grad * gain[None, :]
    proj = lax.optimization_barrier(jnp.mean(inputs * scaled, axis=1, keepdims=True))
    input_grad = out_grad.astype(jnp.float32) + inv_rms * scaled - inputs * inv_rms ** 3 * proj
    input_grad = input_grad.astype(jnp.bfloat16)
    scores = jnp.dot(input_grad, table.T, preferred_element_type=jnp.float32)
    current = jnp.take_along_axis(scores, suffix_ids[:, None].astype(jnp.int32), axis=1)
    return scores - current

def reference(layer_input, norm_gain, w_gate, w_up, hidden_cot, output_cot, embed, suffix_ids):
    total = jnp.zeros((ROWS, VOCAB), jnp.float32)
    for member in range(MEMBERS):
        total = total + member_term(layer_input[member], norm_gain[member], w_gate[member], w_up[member], hidden_cot[member], output_cot[member], embed[member], suffix_ids)
    return total
```

```python
import functools

import jax
import jax.numpy as jnp
from jax import lax
from jax.experimental import pallas as pl
from jax.experimental.pallas import tpu as pltpu
from jax.sharding import PartitionSpec as P

F32 = jnp.float32
BF16 = jnp.bfloat16
NT = (((1,), (1,)), ((), ()))
TN = (((0,), (0,)), ((), ()))
HIGH = lax.Precision.HIGHEST


def grid_of(n):
    inner = 1
    while (2 * inner) ** 3 <= n:
        inner *= 2
    return n // (inner * inner), inner, inner


def kernel(
    n, members, lines, rows, width,
    x_in, gain_in, hid_in, cot_in, ids_in, wg_hbm, wu_hbm, emb_hbm, out_ref,
    xg, gg, part, r1y, r1x, r2x, r2y, r3, st_in, st_sq, st_pr, st_cu,
    wg_v, wu_v, wcat, emb_v, emb3, gain3, hcat, acc, inv_ref, sums, scores, others,
    load_sem, st_send, st_recv, x_send, x_recv, g_send, g_recv,
    s1y, q1y, s1x, q1x, s2, q2x, q2y, s3, q3, m_send, m_recv,
):
    A, B, C = lines
    rp, dl = xg.shape[1], xg.shape[2]
    half = rp // 2
    fl = hid_in.shape[1]
    fp = hcat.shape[1] // 2
    vl = emb_hbm.shape[0]
    me = lax.axis_index("shard")
    mine = lax.axis_index("member")
    c0 = lax.rem(me, C)
    b0 = lax.rem(lax.div(me, C), B)
    a0 = lax.div(me, B * C)

    def at(a, b, c):
        return (a * B + b) * C + c

    def turn(v, d, size):
        return lax.rem(v + d, size)

    def remote(src, dst, send, recv, peer, axis="shard"):
        return pltpu.make_async_remote_copy(
            src_ref=src, dst_ref=dst, send_sem=send, recv_sem=recv,
            device_id={axis: peer}, device_id_type=pl.DeviceIdType.MESH,
        )

    loads = [
        pltpu.make_async_copy(wg_hbm, wg_v, load_sem.at[0]),
        pltpu.make_async_copy(wu_hbm, wu_v, load_sem.at[1]),
        pltpu.make_async_copy(emb_hbm, emb_v, load_sem.at[2]),
    ]
    for load in loads:
        load.start()

    barrier = pltpu.get_barrier_semaphore()
    for d in range(1, n):
        pl.semaphore_signal(barrier, inc=1, device_id={"shard": turn(me, d, n)},
                            device_id_type=pl.DeviceIdType.MESH)
    for d in range(1, members):
        pl.semaphore_signal(barrier, inc=1, device_id={"member": turn(mine, d, members)},
                            device_id_type=pl.DeviceIdType.MESH)

    xg[me] = jnp.zeros((rp, dl), BF16)
    xg[me, 0:rows, :] = x_in[...]
    x_own = x_in[...].astype(F32)

    def first_row(k):
        return (lax.broadcasted_iota(jnp.int32, (8, k), 0) == 0).astype(F32)

    def to_row(values):
        return lax.dot_general(first_row(values.shape[1]), values, NT, precision=HIGH,
                               preferred_element_type=F32)

    def to_column(row, lanes):
        return lax.dot_general(row, jnp.ones((8, lanes), F32), TN, precision=HIGH,
                               preferred_element_type=F32)

    def stat_copy(k, buf, d):
        return remote(st_in.at[k], buf.at[me], st_send.at[k, d], st_recv.at[k, me], turn(me, d, n))

    def stat_send(k, buf):
        for d in range(1, n):
            stat_copy(k, buf, d).start()

    def stat_sum(k, buf):
        total = st_in[k]
        for d in range(1, n):
            src = turn(me, d, n)
            remote(st_in.at[k], buf.at[src], st_send.at[k, d], st_recv.at[k, src], src).wait_recv()
            total = total + buf[src]
        for d in range(1, n):
            stat_copy(k, buf, d).wait_send()
        return total

    pad = jnp.zeros((rp - rows, dl), F32)
    st_in[0] = to_row(jnp.concatenate([x_own * x_own, pad], axis=0))
    pl.semaphore_wait(barrier, n - 1 + members - 1)

    def gather(buf, send, recv, before, process):
        per = (B - 1) + (C - 1) + 2 * (B - 1) * (C - 1)

        def line(blk, index, peer):
            return remote(buf.at[blk], buf.at[blk], send.at[index], recv.at[blk, 0], peer)

        def piece(blk, index, peer, h):
            view = buf.at[blk, pl.ds(h * half, half)]
            return remote(view, view, send.at[index], recv.at[blk, h], peer)

        def outs(da):
            a = turn(a0, da, A)
            base = (A - 1) + da * per
            full, low, high = [], [], []
            k = 0
            for db in range(1, B):
                full.append(line(at(a, b0, c0), base + k, at(a0, turn(b0, db, B), c0)))
                k += 1
            for dc in range(1, C):
                full.append(line(at(a, b0, c0), base + k, at(a0, b0, turn(c0, dc, C))))
                k += 1
            for dc in range(1, C):
                for db in range(1, B):
                    low.append(piece(at(a, b0, turn(c0, dc, C)), base + k,
                                     at(a0, turn(b0, db, B), c0), 0))
                    k += 1
            for db in range(1, B):
                for dc in range(1, C):
                    high.append(piece(at(a, turn(b0, db, B), c0), base + k,
                                      at(a0, b0, turn(c0, dc, C)), 1))
                    k += 1
            return full, low, high

        def outer(da):
            return line(me, da - 1, at(turn(a0, da, A), b0, c0))

        for copy in outs(0)[0]:
            copy.start()
        for da in range(1, A):
            outer(da).start()
        before()

        def step(t, carry):
            @pl.when(jnp.logical_and(t >= 1, t < A))
            def _():
                src = at(turn(a0, t, A), b0, c0)
                line(src, 0, src).wait_recv()
                for copy in outs(t)[0]:
                    copy.start()

            @pl.when(jnp.logical_and(t >= 1, t < A + 1))
            def _():
                da = t - 1
                a = turn(a0, da, A)
                _, low, high = outs(da)
                xs = [at(a, b0, turn(c0, dc, C)) for dc in range(1, C)]
                ys = [at(a, turn(b0, db, B), c0) for db in range(1, B)]
                for i, blk in enumerate(xs):
                    line(blk, 0, at(a0, b0, turn(c0, i + 1, C))).wait_recv()
                    for copy in low[i * (B - 1):(i + 1) * (B - 1)]:
                        copy.start()
                for i, blk in enumerate(ys):
                    line(blk, 0, at(a0, turn(b0, i + 1, B), c0)).wait_recv()
                    for copy in high[i * (C - 1):(i + 1) * (C - 1)]:
                        copy.start()
                for blk in [at(a, b0, c0)] + xs + ys:
                    process(blk)

            @pl.when(t >= 2)
            def _():
                a = turn(a0, t - 2, A)
                for db in range(1, B):
                    for dc in range(1, C):
                        b, c = turn(b0, db, B), turn(c0, dc, C)
                        piece(at(a, b, c), 0, at(a0, b, c0), 0).wait_recv()
                        piece(at(a, b, c), 0, at(a0, b0, c), 1).wait_recv()
                        process(at(a, b, c))

            return carry

        lax.fori_loop(0, A + 2, step, 0)

        for da in range(1, A):
            outer(da).wait_send()

        def done(da, carry):
            full, low, high = outs(da)
            for copy in full + low + high:
                copy.wait_send()
            return carry

        lax.fori_loop(0, A, done, 0)

    stat_send(0, st_sq)

    def prepare():
        for b in range(n):
            gain3[b] = gain_in[:, b * dl:(b + 1) * dl]
        wcat[...] = jnp.zeros_like(wcat)
        loads[0].wait()
        wcat[:, 0:fl] = wg_v[...]
        loads[1].wait()
        wcat[:, fp:fp + fl] = wu_v[...]
        acc[...] = jnp.zeros_like(acc)
        scores[...] = jnp.zeros_like(scores)
        square = to_column(stat_sum(0, st_sq), 128)
        inv_ref[...] = 1.0 / jnp.sqrt(square / width + 1e-05)

    def up(blk):
        x = xg[blk].astype(F32)
        normed = (x * inv_ref[:, 0:1] * gain3[blk]).astype(BF16)
        w = wcat[pl.ds(pl.multiple_of(blk * dl, dl), dl), :]
        acc[...] += jnp.dot(normed, w, preferred_element_type=F32)

    gather(xg, x_send, x_recv, prepare, up)

    gate_pre = acc[0:rows, 0:fl]
    up_proj = acc[0:rows, fp:fp + fl]
    hid = hid_in[...].astype(F32)
    s = jax.nn.sigmoid(gate_pre)
    gate_grad = (hid * up_proj * s * (1.0 + gate_pre * (1.0 - s))).astype(BF16)
    up_grad = (hid * gate_pre * s).astype(BF16)
    hcat[...] = jnp.zeros_like(hcat)
    hcat[0:rows, 0:fl] = gate_grad
    hcat[0:rows, fp:fp + fl] = up_grad
    st_in[1] = to_row(hcat[...].astype(F32) * acc[...])
    stat_send(1, st_pr)

    def product(blk):
        w = wcat[pl.ds(pl.multiple_of(blk * dl, dl), dl), :]
        return lax.dot_general(hcat[...], w, NT, preferred_element_type=F32)

    lo, hi = pl.ds(0, half), pl.ds(half, half)

    def first(a):
        copies = []
        for db in range(1, B):
            for dc in range(1, C):
                b, c = turn(b0, db, B), turn(c0, dc, C)
                blk = at(a, b, c)
                copies.append((blk, remote(part.at[blk, lo], r1y.at[a, c, b0],
                                           s1y.at[blk], q1y.at[a, c, b0], at(a0, b, c0))))
                copies.append((blk, remote(part.at[blk, hi], r1x.at[a, b, c0],
                                           s1x.at[blk], q1x.at[a, b, c0], at(a0, b0, c))))
        return copies

    def second(a):
        copies = []
        for dc in range(1, C):
            c = turn(c0, dc, C)
            blk = at(a, b0, c)
            copies.append((blk, c, 0, remote(part.at[blk], r2x.at[a, c0], s2.at[blk],
                                             q2x.at[a, c0], at(a0, b0, c))))
        for db in range(1, B):
            b = turn(b0, db, B)
            blk = at(a, b, c0)
            copies.append((blk, b, 1, remote(part.at[blk], r2y.at[a, b0], s2.at[blk],
                                             q2y.at[a, b0], at(a0, b, c0))))
        return copies

    def third(a):
        blk = at(a, b0, c0)
        return remote(part.at[blk], r3.at[a0], s3.at[a], q3.at[a0], at(a, b0, c0))

    def reduce_step(t, carry):
        @pl.when(t < A)
        def _():
            a = turn(a0, t + 1, A)
            done = None
            for i, (blk, copy) in enumerate(first(a)):
                if i % 2 == 0:
                    part[blk] = product(blk).astype(BF16)
                copy.start()

        @pl.when(jnp.logical_and(t >= 1, t < A + 1))
        def _():
            a = turn(a0, t, A)
            for blk, other, way, copy in second(a):
                value = product(blk)
                if way == 0:
                    edge = value[0:half]
                    for db in range(1, B):
                        b = turn(b0, db, B)
                        slot = r1y.at[a, other, b]
                        remote(slot, slot, s1y.at[blk], q1y.at[a, other, b], at(a0, b, c0)).wait_recv()
                        edge = edge + r1y[a, other, b].astype(F32)
                    part[blk, 0:half] = edge.astype(BF16)
                    part[blk, half:rp] = value[half:rp].astype(BF16)
                else:
                    edge = value[half:rp]
                    for dc in range(1, C):
                        c = turn(c0, dc, C)
                        slot = r1x.at[a, other, c]
                        remote(slot, slot, s1x.at[blk], q1x.at[a, other, c], at(a0, b0, c)).wait_recv()
                        edge = edge + r1x[a, other, c].astype(F32)
                    part[blk, 0:half] = value[0:half].astype(BF16)
                    part[blk, half:rp] = edge.astype(BF16)
                copy.start()

        @pl.when(t >= 2)
        def _():
            a = turn(a0, t - 1, A)
            blk = at(a, b0, c0)
            value = product(blk)
            for dc in range(1, C):
                c = turn(c0, dc, C)
                slot = r2x.at[a, c]
                remote(slot, slot, s2.at[blk], q2x.at[a, c], at(a0, b0, c)).wait_recv()
                value = value + r2x[a, c].astype(F32)
            for db in range(1, B):
                b = turn(b0, db, B)
                slot = r2y.at[a, b]
                remote(slot, slot, s2.at[blk], q2y.at[a, b], at(a0, b, c0)).wait_recv()
                value = value + r2y[a, b].astype(F32)
            sums[...] = value

            @pl.when(t < A + 1)
            def _():
                part[blk] = value.astype(BF16)
                third(a).start()

        return carry

    lax.fori_loop(0, A + 2, reduce_step, 0)

    loads[2].wait()
    for b in range(n):
        emb3[b] = emb_v[:, b * dl:(b + 1) * dl]

    proj = to_column(stat_sum(1, st_pr), 128)
    share = sums[...]
    for da in range(1, A):
        a = turn(a0, da, A)
        remote(r3.at[a], r3.at[a], s3.at[a], q3.at[a], at(a, b0, c0)).wait_recv()
        share = share + r3[a].astype(F32)
    inv = inv_ref[0:rows, 0:1]
    scaled = share[0:rows] * gain3[me]
    grad = cot_in[...].astype(F32) + inv * scaled - x_own * (inv * inv * (proj[0:rows, 0:1] / width))
    gg[me] = jnp.zeros((rp, dl), BF16)
    gg[me, 0:rows, :] = grad.astype(BF16)

    def settle(d, carry):
        a = turn(a0, d, A)
        for _, copy in first(a):
            copy.wait_send()
        for _, _, _, copy in second(a):
            copy.wait_send()

        @pl.when(d >= 1)
        def _():
            third(a).wait_send()

        return carry

    def score(blk):
        scores[...] += lax.dot_general(gg[blk], emb3[blk], NT, preferred_element_type=F32)

    gather(gg, g_send, g_recv, lambda: None, score)
    lax.fori_loop(0, A, settle, 0)

    def member_copy(d):
        return remote(scores, others.at[mine], m_send.at[d], m_recv.at[mine],
                      turn(mine, d, members), "member")

    for d in range(1, members):
        member_copy(d).start()
    ids = to_column(first_row(rp)[:, 0:rows] * ids_in[...].astype(F32), vl)
    entry = (lax.broadcasted_iota(jnp.int32, (rows, vl), 1) + me * vl).astype(F32)
    total = scores[...]
    for d in range(1, members):
        src = turn(mine, d, members)
        remote(others.at[src], others.at[src], m_send.at[d], m_recv.at[src], src, "member").wait_recv()
        total = total + others[src]
    own = jnp.where(ids == entry, total[0:rows], 0.0)
    st_in[2] = to_row(jnp.concatenate([own, jnp.zeros((rp - rows, vl), F32)], axis=0))
    stat_send(2, st_cu)
    current = to_column(stat_sum(2, st_cu), 128)
    out_ref[...] = total[0:rows] - current[0:rows, 0:1]
    for d in range(1, members):
        member_copy(d).wait_send()


def on_device(n, members, layer_input, norm_gain, w_gate, w_up, hidden_cot, output_cot, embed, suffix_ids):
    _, rows, dl = layer_input.shape
    width = norm_gain.shape[1]
    fl = w_gate.shape[2]
    vl = embed.shape[1]
    lines = A, B, C = grid_of(n)
    rp = -(-rows // 32) * 32
    fp = -(-fl // 128) * 128
    half = rp // 2
    per = (B - 1) + (C - 1) + 2 * (B - 1) * (C - 1)
    moves = (A - 1) + A * per
    vmem = pl.BlockSpec(memory_space=pltpu.VMEM)
    hbm = pl.BlockSpec(memory_space=pl.ANY)
    dma = pltpu.SemaphoreType.DMA
    V = pltpu.VMEM
    scratch = [
        V((n, rp, dl), BF16), V((n, rp, dl), BF16), V((n, rp, dl), BF16),
        V((A, C, B, half, dl), BF16), V((A, B, C, half, dl), BF16),
        V((A, C, rp, dl), BF16), V((A, B, rp, dl), BF16), V((A, rp, dl), BF16),
        V((3, 8, rp), F32), V((n, 8, rp), F32), V((n, 8, rp), F32), V((n, 8, rp), F32),
        V((width, fl), BF16), V((width, fl), BF16), V((width, 2 * fp), BF16),
        V((vl, width), BF16), V((n, vl, dl), BF16), V((n, 1, dl), F32),
        V((rp, 2 * fp), BF16), V((rp, 2 * fp), F32), V((rp, 128), F32), V((rp, dl), F32),
        V((rp, vl), F32), V((members, rp, vl), F32),
        dma((3,)), dma((3, n)), dma((3, n)), dma((moves,)), dma((n, 2)), dma((moves,)), dma((n, 2)),
        dma((n,)), dma((A, C, B)), dma((n,)), dma((A, B, C)), dma((n,)), dma((A, C)), dma((A, B)),
        dma((A,)), dma((A,)), dma((members,)), dma((members,)),
    ]
    return pl.pallas_call(
        functools.partial(kernel, n, members, lines, rows, width),
        out_shape=jax.ShapeDtypeStruct((rows, vl), F32),
        in_specs=[vmem] * 5 + [hbm] * 3,
        out_specs=vmem,
        scratch_shapes=scratch,
        compiler_params=pltpu.CompilerParams(
            collective_id=0, has_side_effects=True, vmem_limit_bytes=56 * 1024 * 1024
        ),
    )(layer_input[0], norm_gain, hidden_cot[0], output_cot[0], suffix_ids[None, :],
      w_gate[0], w_up[0], embed[0])


def solution(mesh):
    n, members = mesh.shape["shard"], mesh.shape["member"]
    placed = (
        P("member", None, "shard"),
        P("member", None),
        P("member", None, "shard"),
        P("member", None, "shard"),
        P("member", None, "shard"),
        P("member", None, "shard"),
        P("member", "shard", None),
        P(),
    )
    return jax.shard_map(
        functools.partial(on_device, n, members),
        mesh=mesh, in_specs=placed, out_specs=P(None, "shard"), check_vma=False,
    )
```

```python
import functools

import jax
import jax.numpy as jnp
from jax import lax
from jax.experimental import pallas as pl
from jax.experimental.pallas import tpu as pltpu
from jax.sharding import PartitionSpec as P

F32 = jnp.float32
BF16 = jnp.bfloat16
NT = (((1,), (1,)), ((), ()))
TN = (((0,), (0,)), ((), ()))
HIGH = lax.Precision.HIGHEST


def grid_of(n):
    inner = 1
    while (2 * inner) ** 3 <= n:
        inner *= 2
    return n // (inner * inner), inner, inner


def pack(value):
    rp, dl = value.shape
    q, r = divmod(dl, 128)
    pieces = [value[:, k * 128:(k + 1) * 128] for k in range(q)]
    if r:
        tail = value[:, q * 128:]
        if r <= 64:
            tail = jnp.concatenate([tail, jnp.zeros((rp, 64 - r), tail.dtype)], axis=1) if r < 64 else tail
            tail = jnp.concatenate([tail[:rp // 2], tail[rp // 2:]], axis=1)
        else:
            tail = jnp.concatenate([tail, jnp.zeros((rp, 128 - r), tail.dtype)], axis=1)
        pieces.append(tail)
    return jnp.concatenate(pieces, axis=0) if len(pieces) > 1 else pieces[0]


def unpack(packed, rp, dl):
    q, r = divmod(dl, 128)
    pieces = [packed[k * rp:(k + 1) * rp] for k in range(q)]
    if r:
        tail = packed[q * rp:]
        if r <= 64:
            tail = jnp.concatenate([tail[:, :r], tail[:, 64:64 + r]], axis=0)
        else:
            tail = tail[:, :r]
        pieces.append(tail)
    return jnp.concatenate(pieces, axis=1) if len(pieces) > 1 else pieces[0]


def kernel(
    n, members, lines, rows, width,
    x_in, gain_in, hid_in, cot_in, ids_in, wg_hbm, wu_hbm, emb_hbm, out_ref, cur_ref,
    xg, gg, part, r1y, r1x, r2x, r2y, r3, st_in, st_sq, st_pr, st_cu,
    wg_v, wu_v, wt3, emb_v, emb3, gain3, hcat, acc, inv_ref, sums, scores, others,
    load_sem, st_send, st_recv, x_send, x_recv, g_send, g_recv,
    s1y, q1y, s1x, q1x, s2, q2x, q2y, s3, q3, m_send, m_recv,
):
    A, B, C = lines
    dl = x_in.shape[1]
    rp = hcat.shape[0]
    half = xg.shape[1] // 2
    fl = hid_in.shape[1]
    vl = emb_hbm.shape[0]
    me = lax.axis_index("shard")
    mine = lax.axis_index("member")
    c0 = lax.rem(me, C)
    b0 = lax.rem(lax.div(me, C), B)
    a0 = lax.div(me, B * C)

    def at(a, b, c):
        return (a * B + b) * C + c

    def turn(v, d, size):
        if size & (size - 1):
            return lax.rem(v + d, size)
        for k in range(size.bit_length() - 1):
            bit = 2 ** k
            on = (d // bit) % 2 if isinstance(d, int) else lax.rem(lax.div(d, bit), 2)
            v = v + on * (bit - 2 * bit * lax.rem(lax.div(v, bit), 2))
        return v

    def remote(src, dst, send, recv, peer, axis="shard"):
        return pltpu.make_async_remote_copy(
            src_ref=src, dst_ref=dst, send_sem=send, recv_sem=recv,
            device_id={axis: peer}, device_id_type=pl.DeviceIdType.MESH,
        )

    loads = [
        pltpu.make_async_copy(wg_hbm, wg_v, load_sem.at[0]),
        pltpu.make_async_copy(wu_hbm, wu_v, load_sem.at[1]),
        pltpu.make_async_copy(emb_hbm, emb_v, load_sem.at[2]),
    ]
    for load in loads:
        load.start()

    barrier = pltpu.get_barrier_semaphore()
    for d in range(1, n):
        pl.semaphore_signal(barrier, inc=1, device_id={"shard": turn(me, d, n)},
                            device_id_type=pl.DeviceIdType.MESH)
    for d in range(1, members):
        pl.semaphore_signal(barrier, inc=1, device_id={"member": turn(mine, d, members)},
                            device_id_type=pl.DeviceIdType.MESH)

    pad = jnp.zeros((rp - rows, dl), F32)
    x_own = jnp.concatenate([x_in[...].astype(F32), pad], axis=0)
    xg[me] = pack(x_own).astype(BF16)

    def first_row(k):
        return (lax.broadcasted_iota(jnp.int32, (8, k), 0) == 0).astype(F32)

    def to_row(values):
        return lax.dot_general(first_row(values.shape[1]), values, NT, precision=HIGH,
                               preferred_element_type=F32)

    def to_column(row, lanes):
        return lax.dot_general(row, jnp.ones((8, lanes), F32), TN, precision=HIGH,
                               preferred_element_type=F32)

    def stat_copy(k, buf, d):
        return remote(st_in.at[k], buf.at[me], st_send.at[k, d], st_recv.at[k, me], turn(me, d, n))

    def stat_send(k, buf):
        for d in range(1, n):
            stat_copy(k, buf, d).start()

    def stat_sum(k, buf):
        total = st_in[k]
        for d in range(1, n):
            src = turn(me, d, n)
            remote(st_in.at[k], buf.at[src], st_send.at[k, d], st_recv.at[k, src], src).wait_recv()
            total = total + buf[src]
        for d in range(1, n):
            stat_copy(k, buf, d).wait_send()
        return total

    st_in[0] = to_row(x_own * x_own)
    pl.semaphore_wait(barrier, n - 1 + members - 1)

    def gather(buf, send, recv, before, process):
        per = (B - 1) + (C - 1) + 2 * (B - 1) * (C - 1)

        def line(blk, index, peer):
            return remote(buf.at[blk], buf.at[blk], send.at[index], recv.at[blk, 0], peer)

        def piece(blk, index, peer, h):
            view = buf.at[blk, pl.ds(h * half, half)]
            return remote(view, view, send.at[index], recv.at[blk, h], peer)

        def outs(da):
            a = turn(a0, da, A)
            base = (A - 1) + da * per
            full, low, high = [], [], []
            k = 0
            for db in range(1, B):
                full.append(line(at(a, b0, c0), base + k, at(a0, turn(b0, db, B), c0)))
                k += 1
            for dc in range(1, C):
                full.append(line(at(a, b0, c0), base + k, at(a0, b0, turn(c0, dc, C))))
                k += 1
            for dc in range(1, C):
                for db in range(1, B):
                    low.append(piece(at(a, b0, turn(c0, dc, C)), base + k,
                                     at(a0, turn(b0, db, B), c0), 0))
                    k += 1
            for db in range(1, B):
                for dc in range(1, C):
                    high.append(piece(at(a, turn(b0, db, B), c0), base + k,
                                      at(a0, b0, turn(c0, dc, C)), 1))
                    k += 1
            return full, low, high

        def outer(da):
            return line(me, da - 1, at(turn(a0, da, A), b0, c0))

        for copy in outs(0)[0]:
            copy.start()
        for da in range(1, A):
            outer(da).start()
        before()

        def step(t, carry):
            @pl.when(jnp.logical_and(t >= 1, t < A))
            def _():
                src = at(turn(a0, t, A), b0, c0)
                line(src, 0, src).wait_recv()
                for copy in outs(t)[0]:
                    copy.start()

            @pl.when(jnp.logical_and(t >= 1, t < A + 1))
            def _():
                da = t - 1
                a = turn(a0, da, A)
                _, low, high = outs(da)
                xs = [at(a, b0, turn(c0, dc, C)) for dc in range(1, C)]
                ys = [at(a, turn(b0, db, B), c0) for db in range(1, B)]
                for i, blk in enumerate(xs):
                    line(blk, 0, at(a0, b0, turn(c0, i + 1, C))).wait_recv()
                    for copy in low[i * (B - 1):(i + 1) * (B - 1)]:
                        copy.start()
                for i, blk in enumerate(ys):
                    line(blk, 0, at(a0, turn(b0, i + 1, B), c0)).wait_recv()
                    for copy in high[i * (C - 1):(i + 1) * (C - 1)]:
                        copy.start()
                for blk in [at(a, b0, c0)] + xs + ys:
                    process(blk)

            @pl.when(t >= 2)
            def _():
                a = turn(a0, t - 2, A)
                for db in range(1, B):
                    for dc in range(1, C):
                        b, c = turn(b0, db, B), turn(c0, dc, C)
                        piece(at(a, b, c), 0, at(a0, b, c0), 0).wait_recv()
                        piece(at(a, b, c), 0, at(a0, b0, c), 1).wait_recv()
                        process(at(a, b, c))

            return carry

        lax.fori_loop(0, A + 2, step, 0)

        for da in range(1, A):
            outer(da).wait_send()

        def done(da, carry):
            full, low, high = outs(da)
            for copy in full + low + high:
                copy.wait_send()
            return carry

        lax.fori_loop(0, A, done, 0)

    stat_send(0, st_sq)

    def prepare():
        for b in range(n):
            gain3[b] = gain_in[:, b * dl:(b + 1) * dl]
        loads[0].wait()
        loads[1].wait()
        for b in range(n):
            wt3[b, 0:fl] = wg_v[:, b * dl:(b + 1) * dl]
            wt3[b, fl:2 * fl] = wu_v[:, b * dl:(b + 1) * dl]
        acc[...] = jnp.zeros_like(acc)
        scores[...] = jnp.zeros_like(scores)
        square = to_column(stat_sum(0, st_sq), 128)
        inv_ref[...] = 1.0 / jnp.sqrt(square / width + 1e-05)

    def up(blk):
        x = unpack(xg[blk].astype(F32), rp, dl)
        normed = (x * inv_ref[:, 0:1] * gain3[blk]).astype(BF16)
        acc[...] += lax.dot_general(normed, wt3[blk], NT, preferred_element_type=F32)

    gather(xg, x_send, x_recv, prepare, up)

    gate_pre = acc[0:rows, 0:fl]
    up_proj = acc[0:rows, fl:2 * fl]
    hid = hid_in[...].astype(F32)
    s = jax.nn.sigmoid(gate_pre)
    gate_grad = (hid * up_proj * s * (1.0 + gate_pre * (1.0 - s))).astype(BF16)
    up_grad = (hid * gate_pre * s).astype(BF16)
    hcat[...] = jnp.zeros_like(hcat)
    hcat[0:rows, 0:fl] = gate_grad
    hcat[0:rows, fl:2 * fl] = up_grad
    st_in[1] = to_row(hcat[...].astype(F32) * acc[...])
    stat_send(1, st_pr)

    def product(blk):
        return pack(jnp.dot(hcat[...], wt3[blk], preferred_element_type=F32))

    lo, hi = pl.ds(0, half), pl.ds(half, half)

    def first(a):
        copies = []
        for db in range(1, B):
            for dc in range(1, C):
                b, c = turn(b0, db, B), turn(c0, dc, C)
                blk = at(a, b, c)
                copies.append((blk, remote(part.at[blk, lo], r1y.at[a, c, b0],
                                           s1y.at[blk], q1y.at[a, c, b0], at(a0, b, c0))))
                copies.append((blk, remote(part.at[blk, hi], r1x.at[a, b, c0],
                                           s1x.at[blk], q1x.at[a, b, c0], at(a0, b0, c))))
        return copies

    def second(a):
        copies = []
        for dc in range(1, C):
            c = turn(c0, dc, C)
            blk = at(a, b0, c)
            copies.append((blk, c, 0, remote(part.at[blk], r2x.at[a, c0], s2.at[blk],
                                             q2x.at[a, c0], at(a0, b0, c))))
        for db in range(1, B):
            b = turn(b0, db, B)
            blk = at(a, b, c0)
            copies.append((blk, b, 1, remote(part.at[blk], r2y.at[a, b0], s2.at[blk],
                                             q2y.at[a, b0], at(a0, b, c0))))
        return copies

    def third(a):
        blk = at(a, b0, c0)
        return remote(part.at[blk], r3.at[a0], s3.at[a], q3.at[a0], at(a, b0, c0))

    def reduce_step(t, carry):
        @pl.when(t < A)
        def _():
            a = turn(a0, lax.rem(t + 1, A), A)
            for i, (blk, copy) in enumerate(first(a)):
                if i % 2 == 0:
                    part[blk] = product(blk).astype(BF16)
                copy.start()

        @pl.when(jnp.logical_and(t >= 1, t < A + 1))
        def _():
            a = turn(a0, lax.rem(t, A), A)
            for blk, other, way, copy in second(a):
                value = product(blk)
                if way == 0:
                    edge = value[0:half]
                    for db in range(1, B):
                        b = turn(b0, db, B)
                        slot = r1y.at[a, other, b]
                        remote(slot, slot, s1y.at[blk], q1y.at[a, other, b], at(a0, b, c0)).wait_recv()
                        edge = edge + r1y[a, other, b].astype(F32)
                    part[blk, 0:half] = edge.astype(BF16)
                    part[blk, half:] = value[half:].astype(BF16)
                else:
                    edge = value[half:]
                    for dc in range(1, C):
                        c = turn(c0, dc, C)
                        slot = r1x.at[a, other, c]
                        remote(slot, slot, s1x.at[blk], q1x.at[a, other, c], at(a0, b0, c)).wait_recv()
                        edge = edge + r1x[a, other, c].astype(F32)
                    part[blk, 0:half] = value[0:half].astype(BF16)
                    part[blk, half:] = edge.astype(BF16)
                copy.start()

        @pl.when(t >= 2)
        def _():
            a = turn(a0, t - 1, A)
            blk = at(a, b0, c0)
            value = product(blk)
            for dc in range(1, C):
                c = turn(c0, dc, C)
                slot = r2x.at[a, c]
                remote(slot, slot, s2.at[blk], q2x.at[a, c], at(a0, b0, c)).wait_recv()
                value = value + r2x[a, c].astype(F32)
            for db in range(1, B):
                b = turn(b0, db, B)
                slot = r2y.at[a, b]
                remote(slot, slot, s2.at[blk], q2y.at[a, b], at(a0, b, c0)).wait_recv()
                value = value + r2y[a, b].astype(F32)
            sums[...] = value

            @pl.when(t < A + 1)
            def _():
                part[blk] = value.astype(BF16)
                third(a).start()

        return carry

    lax.fori_loop(0, A + 2, reduce_step, 0)

    loads[2].wait()
    for b in range(n):
        emb3[b] = emb_v[:, b * dl:(b + 1) * dl]

    proj = to_column(stat_sum(1, st_pr), 128)
    share = sums[...]
    for da in range(1, A):
        a = turn(a0, da, A)
        remote(r3.at[a], r3.at[a], s3.at[a], q3.at[a], at(a, b0, c0)).wait_recv()
        share = share + r3[a].astype(F32)
    inv = inv_ref[:, 0:1]
    scaled = unpack(share, rp, dl) * gain3[me]
    cot = jnp.concatenate([cot_in[...].astype(F32), pad], axis=0)
    grad = cot + inv * scaled - x_own * (inv * inv * (proj[:, 0:1] / width))
    gg[me] = pack(grad).astype(BF16)

    def settle(d, carry):
        a = turn(a0, d, A)
        for _, copy in first(a):
            copy.wait_send()
        for _, _, _, copy in second(a):
            copy.wait_send()

        @pl.when(d >= 1)
        def _():
            third(a).wait_send()

        return carry

    def score(blk):
        scores[...] += lax.dot_general(unpack(gg[blk], rp, dl), emb3[blk], NT, preferred_element_type=F32)

    gather(gg, g_send, g_recv, lambda: None, score)
    lax.fori_loop(0, A, settle, 0)

    def member_copy(d):
        return remote(scores, others.at[mine], m_send.at[d], m_recv.at[mine],
                      turn(mine, d, members), "member")

    for d in range(1, members):
        member_copy(d).start()
    ids = to_column(first_row(rp)[:, 0:rows] * ids_in[...].astype(F32), vl)
    entry = (lax.broadcasted_iota(jnp.int32, (rows, vl), 1) + me * vl).astype(F32)
    total = scores[...]
    for d in range(1, members):
        src = turn(mine, d, members)
        remote(others.at[src], others.at[src], m_send.at[d], m_recv.at[src], src, "member").wait_recv()
        total = total + others[src]
    own = jnp.where(ids == entry, total[0:rows], 0.0)
    st_in[2] = to_row(jnp.concatenate([own, jnp.zeros((rp - rows, vl), F32)], axis=0))
    stat_send(2, st_cu)
    current = to_column(stat_sum(2, st_cu), 128)
    out_ref[...] = total[0:rows]
    cur_ref[...] = current[0:rows]
    for d in range(1, members):
        member_copy(d).wait_send()


def on_device(n, members, layer_input, norm_gain, w_gate, w_up, hidden_cot, output_cot, embed, suffix_ids):
    _, rows, dl = layer_input.shape
    width = norm_gain.shape[1]
    fl = w_gate.shape[2]
    vl = embed.shape[1]
    lines = A, B, C = grid_of(n)
    rp = -(-rows // 32) * 32
    q, r = divmod(dl, 128)
    length = q * rp + (0 if r == 0 else rp // 2 if r <= 64 else rp)
    half = length // 2
    per = (B - 1) + (C - 1) + 2 * (B - 1) * (C - 1)
    moves = (A - 1) + A * per
    vmem = pl.BlockSpec(memory_space=pltpu.VMEM)
    hbm = pl.BlockSpec(memory_space=pl.ANY)
    dma = pltpu.SemaphoreType.DMA
    V = pltpu.VMEM
    scratch = [
        V((n, length, 128), BF16), V((n, length, 128), BF16), V((n, length, 128), BF16),
        V((A, C, B, half, 128), BF16), V((A, B, C, half, 128), BF16),
        V((A, C, length, 128), BF16), V((A, B, length, 128), BF16), V((A, length, 128), BF16),
        V((3, 8, rp), F32), V((n, 8, rp), F32), V((n, 8, rp), F32), V((n, 8, rp), F32),
        V((fl, width), BF16), V((fl, width), BF16), V((n, 2 * fl, dl), BF16),
        V((vl, width), BF16), V((n, vl, dl), BF16), V((n, 1, dl), F32),
        V((rp, 2 * fl), BF16), V((rp, 2 * fl), F32), V((rp, 128), F32), V((length, 128), F32),
        V((rp, vl), F32), V((members, rp, vl), F32),
        dma((3,)), dma((3, n)), dma((3, n)), dma((moves,)), dma((n, 2)), dma((moves,)), dma((n, 2)),
        dma((n,)), dma((A, C, B)), dma((n,)), dma((A, B, C)), dma((n,)), dma((A, C)), dma((A, B)),
        dma((A,)), dma((A,)), dma((members,)), dma((members,)),
    ]
    total, current = pl.pallas_call(
        functools.partial(kernel, n, members, lines, rows, width),
        out_shape=(jax.ShapeDtypeStruct((rows, vl), F32), jax.ShapeDtypeStruct((rows, 128), F32)),
        in_specs=[vmem] * 5 + [hbm] * 3,
        out_specs=(vmem, vmem),
        scratch_shapes=scratch,
        compiler_params=pltpu.CompilerParams(
            collective_id=0, has_side_effects=True, vmem_limit_bytes=56 * 1024 * 1024
        ),
    )(layer_input[0], norm_gain, hidden_cot[0], output_cot[0], suffix_ids[None, :],
      w_gate[0].T, w_up[0].T, embed[0])
    return total - current[:, 0:1]


def solution(mesh):
    n, members = mesh.shape["shard"], mesh.shape["member"]
    placed = (
        P("member", None, "shard"),
        P("member", None),
        P("member", None, "shard"),
        P("member", None, "shard"),
        P("member", None, "shard"),
        P("member", None, "shard"),
        P("member", "shard", None),
        P(),
    )
    return jax.shard_map(
        functools.partial(on_device, n, members),
        mesh=mesh, in_specs=placed, out_specs=P(None, "shard"), check_vma=False,
    )
```

```python
import functools

import jax
import jax.numpy as jnp
from jax import lax
from jax.experimental import pallas as pl
from jax.experimental.pallas import tpu as pltpu
from jax.sharding import PartitionSpec as P

F32 = jnp.float32
BF16 = jnp.bfloat16
NT = (((1,), (1,)), ((), ()))
TN = (((0,), (0,)), ((), ()))
HIGH = lax.Precision.HIGHEST


def grid_of(n):
    inner = 1
    while (2 * inner) ** 3 <= n:
        inner *= 2
    return n // (inner * inner), inner, inner


def pack(value):
    rp, dl = value.shape
    q, r = divmod(dl, 128)
    pieces = [value[:, k * 128:(k + 1) * 128] for k in range(q)]
    if r:
        tail = value[:, q * 128:]
        if r <= 64:
            tail = jnp.concatenate([tail, jnp.zeros((rp, 64 - r), tail.dtype)], axis=1) if r < 64 else tail
            tail = jnp.concatenate([tail[:rp // 2], tail[rp // 2:]], axis=1)
        else:
            tail = jnp.concatenate([tail, jnp.zeros((rp, 128 - r), tail.dtype)], axis=1)
        pieces.append(tail)
    return jnp.concatenate(pieces, axis=0) if len(pieces) > 1 else pieces[0]


def unpack(packed, rp, dl):
    q, r = divmod(dl, 128)
    pieces = [packed[k * rp:(k + 1) * rp] for k in range(q)]
    if r:
        tail = packed[q * rp:]
        if r <= 64:
            tail = jnp.concatenate([tail[:, :r], tail[:, 64:64 + r]], axis=0)
        else:
            tail = tail[:, :r]
        pieces.append(tail)
    return jnp.concatenate(pieces, axis=1) if len(pieces) > 1 else pieces[0]


def kernel(
    n, members, lines, rows, width,
    x_in, gain_in, hid_in, cot_in, ids_in, wg_hbm, wu_hbm, emb_hbm, out_ref,
    xg, gg, part, r1y, r1x, r2x, r2y, r3, st_in, st_sq, st_pr, st_cu,
    wg_v, wu_v, wt3, emb_v, emb3, gain3, hcat, acc, inv_ref, sums, kept, scores, others,
    load_sem, st_send, st_recv, x_send, x_recv, g_send, g_recv,
    s1y, q1y, s1x, q1x, s2, q2x, q2y, s3, q3, m_send, m_recv,
):
    A, B, C = lines
    dl = x_in.shape[1]
    rp = hcat.shape[0]
    half = xg.shape[1] // 2
    fl = hid_in.shape[1]
    vl = emb_hbm.shape[0]
    me = lax.axis_index("shard")
    mine = lax.axis_index("member")
    c0 = lax.rem(me, C)
    b0 = lax.rem(lax.div(me, C), B)
    a0 = lax.div(me, B * C)

    def at(a, b, c):
        return (a * B + b) * C + c

    def turn(v, d, size):
        if size & (size - 1):
            return lax.rem(v + d, size)
        for k in range(size.bit_length() - 1):
            bit = 2 ** k
            on = (d // bit) % 2 if isinstance(d, int) else lax.rem(lax.div(d, bit), 2)
            v = v + on * (bit - 2 * bit * lax.rem(lax.div(v, bit), 2))
        return v

    def remote(src, dst, send, recv, peer, axis="shard"):
        return pltpu.make_async_remote_copy(
            src_ref=src, dst_ref=dst, send_sem=send, recv_sem=recv,
            device_id={axis: peer}, device_id_type=pl.DeviceIdType.MESH,
        )

    loads = [
        pltpu.make_async_copy(wg_hbm, wg_v, load_sem.at[0]),
        pltpu.make_async_copy(wu_hbm, wu_v, load_sem.at[1]),
        pltpu.make_async_copy(emb_hbm, emb_v, load_sem.at[2]),
    ]
    for load in loads:
        load.start()

    barrier = pltpu.get_barrier_semaphore()
    for d in range(1, n):
        pl.semaphore_signal(barrier, inc=1, device_id={"shard": turn(me, d, n)},
                            device_id_type=pl.DeviceIdType.MESH)
    for d in range(1, members):
        pl.semaphore_signal(barrier, inc=1, device_id={"member": turn(mine, d, members)},
                            device_id_type=pl.DeviceIdType.MESH)

    pad = jnp.zeros((rp - rows, dl), F32)
    x_own = jnp.concatenate([x_in[...].astype(F32), pad], axis=0)
    xg[me] = pack(x_own).astype(BF16)

    def first_row(k):
        return (lax.broadcasted_iota(jnp.int32, (8, k), 0) == 0).astype(F32)

    def to_row(values):
        return lax.dot_general(first_row(values.shape[1]), values, NT, precision=HIGH,
                               preferred_element_type=F32)[0:1]

    def to_column(row, lanes):
        rows8 = first_row(row.shape[1]) * row
        return lax.dot_general(rows8, jnp.ones((8, lanes), F32), TN, precision=HIGH,
                               preferred_element_type=F32)

    def stat_copy(k, buf, d):
        return remote(st_in.at[k], buf.at[me], st_send.at[k, d], st_recv.at[k, me], turn(me, d, n))

    def stat_send(k, buf):
        for d in range(1, n):
            stat_copy(k, buf, d).start()

    def stat_sum(k, buf):
        total = st_in[k]
        for d in range(1, n):
            src = turn(me, d, n)
            remote(st_in.at[k], buf.at[src], st_send.at[k, d], st_recv.at[k, src], src).wait_recv()
            total = total + buf[src]
        for d in range(1, n):
            stat_copy(k, buf, d).wait_send()
        return total

    st_in[0] = to_row(x_own * x_own)
    pl.semaphore_wait(barrier, n - 1 + members - 1)

    def gather(buf, send, recv, before, process):
        per = 2 * (B - 1) + 2 * (C - 1) + 2 * (B - 1) * (C - 1)

        def piece(blk, h, index, peer):
            view = buf.at[blk, pl.ds(h * half, half)]
            return remote(view, view, send.at[index], recv.at[blk, h], peer)

        def outs(da):
            a = turn(a0, da, A)
            base = 2 * (A - 1) + da * per
            full, low, high = ([], []), [], []
            k = 0
            for h in (0, 1):
                for dc in range(1, C):
                    full[h].append(piece(at(a, b0, c0), h, base + k, at(a0, b0, turn(c0, dc, C))))
                    k += 1
                for db in range(1, B):
                    full[h].append(piece(at(a, b0, c0), h, base + k, at(a0, turn(b0, db, B), c0)))
                    k += 1
            for dc in range(1, C):
                for db in range(1, B):
                    low.append(piece(at(a, b0, turn(c0, dc, C)), 0, base + k,
                                     at(a0, turn(b0, db, B), c0)))
                    k += 1
            for db in range(1, B):
                for dc in range(1, C):
                    high.append(piece(at(a, turn(b0, db, B), c0), 1, base + k,
                                      at(a0, b0, turn(c0, dc, C))))
                    k += 1
            return full, low, high

        def outer(da, h):
            return piece(me, h, 2 * (da - 1) + h, at(turn(a0, da, A), b0, c0))

        own = outs(0)[0]
        for h in (0, 1):
            for copy in own[h][:C - 1] + own[1 - h][C - 1:]:
                copy.start()
        for da in range(1, A):
            for h in (0, 1):
                outer(da, h).start()
        before()

        def step(t, carry):
            @pl.when(jnp.logical_and(t >= 1, t < A))
            def _():
                src = at(turn(a0, t, A), b0, c0)
                full = outs(t)[0]
                for h in (0, 1):
                    piece(src, h, 0, src).wait_recv()
                    for copy in full[h]:
                        copy.start()

            @pl.when(jnp.logical_and(t >= 1, t < A + 1))
            def _():
                a = turn(a0, t - 1, A)
                _, low, high = outs(t - 1)
                for i in range(C - 1):
                    c = turn(c0, i + 1, C)
                    piece(at(a, b0, c), 0, 0, at(a0, b0, c)).wait_recv()
                    for copy in low[i * (B - 1):(i + 1) * (B - 1)]:
                        copy.start()
                for i in range(B - 1):
                    b = turn(b0, i + 1, B)
                    piece(at(a, b, c0), 1, 0, at(a0, b, c0)).wait_recv()
                    for copy in high[i * (C - 1):(i + 1) * (C - 1)]:
                        copy.start()
                process(at(a, b0, c0))

            @pl.when(t >= 2)
            def _():
                a = turn(a0, t - 2, A)
                for dc in range(1, C):
                    c = turn(c0, dc, C)
                    piece(at(a, b0, c), 1, 0, at(a0, b0, c)).wait_recv()
                    process(at(a, b0, c))
                for db in range(1, B):
                    b = turn(b0, db, B)
                    piece(at(a, b, c0), 0, 0, at(a0, b, c0)).wait_recv()
                    process(at(a, b, c0))
                for db in range(1, B):
                    for dc in range(1, C):
                        b, c = turn(b0, db, B), turn(c0, dc, C)
                        piece(at(a, b, c), 0, 0, at(a0, b, c0)).wait_recv()
                        piece(at(a, b, c), 1, 0, at(a0, b0, c)).wait_recv()
                        process(at(a, b, c))

            return carry

        lax.fori_loop(0, A + 2, step, 0)

        for da in range(1, A):
            for h in (0, 1):
                outer(da, h).wait_send()

        def done(da, carry):
            full, low, high = outs(da)
            for copy in full[0] + full[1] + low + high:
                copy.wait_send()
            return carry

        lax.fori_loop(0, A, done, 0)

    stat_send(0, st_sq)

    def prepare():
        for b in range(n):
            gain3[b] = gain_in[:, b * dl:(b + 1) * dl]
        loads[0].wait()
        loads[1].wait()
        for b in range(n):
            wt3[b, 0:fl] = wg_v[:, b * dl:(b + 1) * dl]
            wt3[b, fl:2 * fl] = wu_v[:, b * dl:(b + 1) * dl]
        acc[...] = jnp.zeros_like(acc)
        scores[...] = jnp.zeros_like(scores)
        square = to_column(stat_sum(0, st_sq), 128)
        inv_ref[...] = 1.0 / jnp.sqrt(square / width + 1e-05)

    def up(blk):
        x = unpack(xg[blk].astype(F32), rp, dl)
        normed = (x * inv_ref[:, 0:1] * gain3[blk]).astype(BF16)
        acc[...] += lax.dot_general(normed, wt3[blk], NT, preferred_element_type=F32)

    gather(xg, x_send, x_recv, prepare, up)

    gate_pre = acc[0:rows, 0:fl]
    up_proj = acc[0:rows, fl:2 * fl]
    hid = hid_in[...].astype(F32)
    s = jax.nn.sigmoid(gate_pre)
    gate_grad = (hid * up_proj * s * (1.0 + gate_pre * (1.0 - s))).astype(BF16)
    up_grad = (hid * gate_pre * s).astype(BF16)
    hcat[...] = jnp.zeros_like(hcat)
    hcat[0:rows, 0:fl] = gate_grad
    hcat[0:rows, fl:2 * fl] = up_grad
    st_in[1] = to_row(hcat[...].astype(F32) * acc[...])
    stat_send(1, st_pr)

    def product(blk):
        return pack(jnp.dot(hcat[...], wt3[blk], preferred_element_type=F32))

    lo, hi = pl.ds(0, half), pl.ds(half, half)

    def first(a):
        copies = []
        for db in range(1, B):
            for dc in range(1, C):
                b, c = turn(b0, db, B), turn(c0, dc, C)
                blk = at(a, b, c)
                copies.append((blk, remote(part.at[blk, lo], r1y.at[a, c, b0],
                                           s1y.at[blk], q1y.at[a, c, b0], at(a0, b, c0))))
                copies.append((blk, remote(part.at[blk, hi], r1x.at[a, b, c0],
                                           s1x.at[blk], q1x.at[a, b, c0], at(a0, b0, c))))
        return copies

    def second(a):
        copies = []
        for dc in range(1, C):
            c = turn(c0, dc, C)
            blk = at(a, b0, c)
            pair = [remote(part.at[blk, span], r2x.at[a, c0, span], s2.at[blk, h],
                           q2x.at[a, c0, h], at(a0, b0, c)) for h, span in ((1, hi), (0, lo))]
            copies.append((blk, c, 0, pair))
        for db in range(1, B):
            b = turn(b0, db, B)
            blk = at(a, b, c0)
            pair = [remote(part.at[blk, span], r2y.at[a, b0, span], s2.at[blk, h],
                           q2y.at[a, b0, h], at(a0, b, c0)) for h, span in ((0, lo), (1, hi))]
            copies.append((blk, b, 1, pair))
        return copies

    def third(a, h):
        blk = at(a, b0, c0)
        span = (lo, hi)[h]
        return remote(part.at[blk, span], r3.at[a0, span], s3.at[a, h], q3.at[a0, h], at(a, b0, c0))

    def reduce_step(t, carry):
        @pl.when(t < A)
        def _():
            a = turn(a0, lax.rem(t + 1, A), A)
            for i, (blk, copy) in enumerate(first(a)):
                if i % 2 == 0:
                    part[blk] = product(blk).astype(BF16)
                copy.start()
            for i, (blk, _, way, pair) in enumerate(second(a)):
                value = product(blk)
                if way == 0:
                    part[blk, half:] = value[half:].astype(BF16)
                    kept[lax.rem(t, 2), i] = value[:half]
                else:
                    part[blk, :half] = value[:half].astype(BF16)
                    kept[lax.rem(t, 2), i] = value[half:]
                pair[0].start()

        @pl.when(jnp.logical_and(t >= 1, t < A + 1))
        def _():
            a = turn(a0, lax.rem(t, A), A)
            for i, (blk, other, way, pair) in enumerate(second(a)):
                edge = kept[lax.rem(t - 1, 2), i]
                if way == 0:
                    for db in range(1, B):
                        b = turn(b0, db, B)
                        slot = r1y.at[a, other, b]
                        remote(slot, slot, s1y.at[blk], q1y.at[a, other, b], at(a0, b, c0)).wait_recv()
                        edge = edge + r1y[a, other, b].astype(F32)
                    part[blk, :half] = edge.astype(BF16)
                else:
                    for dc in range(1, C):
                        c = turn(c0, dc, C)
                        slot = r1x.at[a, other, c]
                        remote(slot, slot, s1x.at[blk], q1x.at[a, other, c], at(a0, b0, c)).wait_recv()
                        edge = edge + r1x[a, other, c].astype(F32)
                    part[blk, half:] = edge.astype(BF16)
                pair[1].start()

        @pl.when(t >= 2)
        def _():
            a = turn(a0, t - 1, A) if A & (A - 1) else turn(a0, lax.rem(t - 1, A), A)
            blk = at(a, b0, c0)
            sums[...] = product(blk)
            for h, span in ((0, lo), (1, hi)):
                value = sums[span]
                for dc in range(1, C):
                    c = turn(c0, dc, C)
                    slot = r2x.at[a, c, span]
                    remote(slot, slot, s2.at[blk, h], q2x.at[a, c, h], at(a0, b0, c)).wait_recv()
                    value = value + r2x[a, c, span].astype(F32)
                for db in range(1, B):
                    b = turn(b0, db, B)
                    slot = r2y.at[a, b, span]
                    remote(slot, slot, s2.at[blk, h], q2y.at[a, b, h], at(a0, b, c0)).wait_recv()
                    value = value + r2y[a, b, span].astype(F32)
                sums[span] = value

                @pl.when(t < A + 1)
                def _():
                    part[blk, span] = value.astype(BF16)
                    third(a, h).start()

        return carry

    lax.fori_loop(0, A + 2, reduce_step, 0)

    loads[2].wait()
    for b in range(n):
        emb3[b] = emb_v[:, b * dl:(b + 1) * dl]

    proj = to_column(stat_sum(1, st_pr), 128)
    share = sums[...]
    for da in range(1, A):
        a = turn(a0, da, A)
        for h, span in ((0, lo), (1, hi)):
            slot = r3.at[a, span]
            remote(slot, slot, s3.at[a, h], q3.at[a, h], at(a, b0, c0)).wait_recv()
        share = share + r3[a].astype(F32)
    inv = inv_ref[:, 0:1]
    scaled = unpack(share, rp, dl) * gain3[me]
    cot = jnp.concatenate([cot_in[...].astype(F32), pad], axis=0)
    grad = cot + inv * scaled - x_own * (inv * inv * (proj[:, 0:1] / width))
    gg[me] = pack(grad).astype(BF16)

    def settle(d, carry):
        a = turn(a0, d, A)
        for _, copy in first(a):
            copy.wait_send()
        for _, _, _, pair in second(a):
            for copy in pair:
                copy.wait_send()

        @pl.when(d >= 1)
        def _():
            third(a, 0).wait_send()
            third(a, 1).wait_send()

        return carry

    def score(blk):
        scores[...] += lax.dot_general(unpack(gg[blk], rp, dl), emb3[blk], NT, preferred_element_type=F32)

    gather(gg, g_send, g_recv, lambda: None, score)
    lax.fori_loop(0, A, settle, 0)

    def member_copy(d):
        return remote(scores, others.at[mine], m_send.at[d], m_recv.at[mine],
                      turn(mine, d, members), "member")

    for d in range(1, members):
        member_copy(d).start()
    ids = to_column(ids_in[...].astype(F32), vl)
    entry = (lax.broadcasted_iota(jnp.int32, (rows, vl), 1) + me * vl).astype(F32)
    total = scores[...]
    for d in range(1, members):
        src = turn(mine, d, members)
        remote(others.at[src], others.at[src], m_send.at[d], m_recv.at[src], src, "member").wait_recv()
        total = total + others[src]
    own = jnp.where(ids == entry, total[0:rows], 0.0)
    st_in[2] = to_row(jnp.concatenate([own, jnp.zeros((rp - rows, vl), F32)], axis=0))
    stat_send(2, st_cu)
    current = to_column(stat_sum(2, st_cu), 128)
    out_ref[...] = total[0:rows] - current[0:rows, 0:1]
    for d in range(1, members):
        member_copy(d).wait_send()


def on_device(n, members, layer_input, norm_gain, w_gate, w_up, hidden_cot, output_cot, embed, suffix_ids):
    _, rows, dl = layer_input.shape
    width = norm_gain.shape[1]
    fl = w_gate.shape[2]
    vl = embed.shape[1]
    lines = A, B, C = grid_of(n)
    rp = -(-rows // 32) * 32
    q, r = divmod(dl, 128)
    length = q * rp + (0 if r == 0 else rp // 2 if r <= 64 else rp)
    half = length // 2
    per = 2 * (B - 1) + 2 * (C - 1) + 2 * (B - 1) * (C - 1)
    moves = 2 * (A - 1) + A * per
    vmem = pl.BlockSpec(memory_space=pltpu.VMEM)
    hbm = pl.BlockSpec(memory_space=pl.ANY)
    dma = pltpu.SemaphoreType.DMA
    V = pltpu.VMEM
    scratch = [
        V((n, length, 128), BF16), V((n, length, 128), BF16), V((n, length, 128), BF16),
        V((A, C, B, half, 128), BF16), V((A, B, C, half, 128), BF16),
        V((A, C, length, 128), BF16), V((A, B, length, 128), BF16), V((A, length, 128), BF16),
        V((3, 1, rp), F32), V((n, 1, rp), F32), V((n, 1, rp), F32), V((n, 1, rp), F32),
        V((fl, width), BF16), V((fl, width), BF16), V((n, 2 * fl, dl), BF16),
        V((vl, width), BF16), V((n, vl, dl), BF16), V((n, 1, dl), F32),
        V((rp, 2 * fl), BF16), V((rp, 2 * fl), F32), V((rp, 128), F32), V((length, 128), F32),
        V((2, B + C - 2, half, 128), F32),
        V((rp, vl), F32), V((members, rp, vl), F32),
        dma((3,)), dma((3, n)), dma((3, n)), dma((moves,)), dma((n, 2)), dma((moves,)), dma((n, 2)),
        dma((n,)), dma((A, C, B)), dma((n,)), dma((A, B, C)), dma((n, 2)), dma((A, C, 2)), dma((A, B, 2)),
        dma((A, 2)), dma((A, 2)), dma((members,)), dma((members,)),
    ]
    return pl.pallas_call(
        functools.partial(kernel, n, members, lines, rows, width),
        out_shape=jax.ShapeDtypeStruct((rows, vl), F32),
        in_specs=[vmem] * 5 + [hbm] * 3,
        out_specs=vmem,
        scratch_shapes=scratch,
        compiler_params=pltpu.CompilerParams(
            collective_id=0, has_side_effects=True, vmem_limit_bytes=56 * 1024 * 1024
        ),
    )(layer_input[0], norm_gain, hidden_cot[0], output_cot[0], suffix_ids[None, :],
      w_gate[0].T, w_up[0].T, embed[0])


def solution(mesh):
    n, members = mesh.shape["shard"], mesh.shape["member"]
    placed = (
        P("member", None, "shard"),
        P("member", None),
        P("member", None, "shard"),
        P("member", None, "shard"),
        P("member", None, "shard"),
        P("member", None, "shard"),
        P("member", "shard", None),
        P(),
    )
    return jax.shard_map(
        functools.partial(on_device, n, members),
        mesh=mesh, in_specs=placed, out_specs=P(None, "shard"), check_vma=False,
    )
```

```python
import functools

import jax
import jax.numpy as jnp
from jax import lax
from jax.experimental import pallas as pl
from jax.experimental.pallas import tpu as pltpu
from jax.sharding import PartitionSpec as P

F32 = jnp.float32
BF16 = jnp.bfloat16
NT = (((1,), (1,)), ((), ()))
TN = (((0,), (0,)), ((), ()))
HIGH = lax.Precision.HIGHEST


def grid_of(n):
    inner = 1
    while (2 * inner) ** 3 <= n:
        inner *= 2
    return n // (inner * inner), inner, inner


def pack(value):
    rp, dl = value.shape
    q, r = divmod(dl, 128)
    pieces = [value[:, k * 128:(k + 1) * 128] for k in range(q)]
    if r:
        tail = value[:, q * 128:]
        if r <= 64:
            tail = jnp.concatenate([tail, jnp.zeros((rp, 64 - r), tail.dtype)], axis=1) if r < 64 else tail
            tail = jnp.concatenate([tail[:rp // 2], tail[rp // 2:]], axis=1)
        else:
            tail = jnp.concatenate([tail, jnp.zeros((rp, 128 - r), tail.dtype)], axis=1)
        pieces.append(tail)
    return jnp.concatenate(pieces, axis=0) if len(pieces) > 1 else pieces[0]


def unpack(packed, rp, dl):
    q, r = divmod(dl, 128)
    pieces = [packed[k * rp:(k + 1) * rp] for k in range(q)]
    if r:
        tail = packed[q * rp:]
        if r <= 64:
            tail = jnp.concatenate([tail[:, :r], tail[:, 64:64 + r]], axis=0)
        else:
            tail = tail[:, :r]
        pieces.append(tail)
    return jnp.concatenate(pieces, axis=1) if len(pieces) > 1 else pieces[0]


def kernel(
    n, members, lines, rows, width,
    x_in, gain_in, hid_in, cot_in, ids_in, wg_hbm, wu_hbm, emb_hbm, out_ref,
    xg, gg, part, r1y, r1x, r2x, r2y, r3, st_in, st_sq, st_pr, st_cu,
    wg_v, wu_v, wt3, emb_v, emb3, gain3, hcat, acc, inv_ref, sums, kept, scores, others,
    load_sem, st_send, st_recv, x_send, x_recv, g_send, g_recv,
    s1y, q1y, s1x, q1x, s2, q2x, q2y, s3, q3, m_send, m_recv,
):
    A, B, C = lines
    dl = x_in.shape[1]
    rp = hcat.shape[0]
    half = xg.shape[1] // 2
    fl = hid_in.shape[1]
    vl = emb_hbm.shape[0]
    me = lax.axis_index("shard")
    mine = lax.axis_index("member")
    c0 = lax.rem(me, C)
    b0 = lax.rem(lax.div(me, C), B)
    a0 = lax.div(me, B * C)

    def at(a, b, c):
        return (a * B + b) * C + c

    def turn(v, d, size):
        if size & (size - 1):
            return lax.rem(v + d, size)
        for k in range(size.bit_length() - 1):
            bit = 2 ** k
            on = (d // bit) % 2 if isinstance(d, int) else lax.rem(lax.div(d, bit), 2)
            v = v + on * (bit - 2 * bit * lax.rem(lax.div(v, bit), 2))
        return v

    def remote(src, dst, send, recv, peer, axis="shard"):
        return pltpu.make_async_remote_copy(
            src_ref=src, dst_ref=dst, send_sem=send, recv_sem=recv,
            device_id={axis: peer}, device_id_type=pl.DeviceIdType.MESH,
        )

    loads = [
        pltpu.make_async_copy(wg_hbm, wg_v, load_sem.at[0]),
        pltpu.make_async_copy(wu_hbm, wu_v, load_sem.at[1]),
        pltpu.make_async_copy(emb_hbm, emb_v, load_sem.at[2]),
    ]
    for load in loads:
        load.start()

    barrier = pltpu.get_barrier_semaphore()
    for d in range(1, n):
        pl.semaphore_signal(barrier, inc=1, device_id={"shard": turn(me, d, n)},
                            device_id_type=pl.DeviceIdType.MESH)
    for d in range(1, members):
        pl.semaphore_signal(barrier, inc=1, device_id={"member": turn(mine, d, members)},
                            device_id_type=pl.DeviceIdType.MESH)

    pad = jnp.zeros((rp - rows, dl), F32)
    x_own = jnp.concatenate([x_in[...].astype(F32), pad], axis=0)
    xg[me] = pack(x_own).astype(BF16)

    def first_row(k):
        return (lax.broadcasted_iota(jnp.int32, (8, k), 0) == 0).astype(F32)

    def to_row(values):
        return lax.dot_general(first_row(values.shape[1]), values, NT, precision=HIGH,
                               preferred_element_type=F32)[0:1]

    def to_column(row, lanes):
        rows8 = first_row(row.shape[1]) * row
        return lax.dot_general(rows8, jnp.ones((8, lanes), F32), TN, precision=HIGH,
                               preferred_element_type=F32)

    def stat_copy(k, buf, d):
        return remote(st_in.at[k], buf.at[me], st_send.at[k, d], st_recv.at[k, me], turn(me, d, n))

    def stat_send(k, buf):
        for d in range(1, n):
            stat_copy(k, buf, d).start()

    def stat_sum(k, buf):
        total = st_in[k]
        for d in range(1, n):
            src = turn(me, d, n)
            remote(st_in.at[k], buf.at[src], st_send.at[k, d], st_recv.at[k, src], src).wait_recv()
            total = total + buf[src]
        for d in range(1, n):
            stat_copy(k, buf, d).wait_send()
        return total

    st_in[0] = to_row(x_own * x_own)
    for b in range(n):
        gain3[b] = gain_in[:, b * dl:(b + 1) * dl]
    loads[0].wait()
    loads[1].wait()
    for b in range(n):
        wt3[b, 0:fl] = wg_v[:, b * dl:(b + 1) * dl]
        wt3[b, fl:2 * fl] = wu_v[:, b * dl:(b + 1) * dl]
    acc[...] = jnp.zeros_like(acc)
    scores[...] = jnp.zeros_like(scores)
    pl.semaphore_wait(barrier, n - 1 + members - 1)

    def gather(buf, send, recv, before, process, late):
        per = 2 * (B - 1) + 2 * (C - 1) + 2 * (B - 1) * (C - 1)

        def piece(blk, h, index, peer):
            view = buf.at[blk, pl.ds(h * half, half)]
            return remote(view, view, send.at[index], recv.at[blk, h], peer)

        def outs(da):
            a = turn(a0, da, A)
            base = 2 * (A - 1) + da * per
            full, low, high = ([], []), [], []
            k = 0
            for h in (0, 1):
                for dc in range(1, C):
                    full[h].append(piece(at(a, b0, c0), h, base + k, at(a0, b0, turn(c0, dc, C))))
                    k += 1
                for db in range(1, B):
                    full[h].append(piece(at(a, b0, c0), h, base + k, at(a0, turn(b0, db, B), c0)))
                    k += 1
            for dc in range(1, C):
                for db in range(1, B):
                    low.append(piece(at(a, b0, turn(c0, dc, C)), 0, base + k,
                                     at(a0, turn(b0, db, B), c0)))
                    k += 1
            for db in range(1, B):
                for dc in range(1, C):
                    high.append(piece(at(a, turn(b0, db, B), c0), 1, base + k,
                                      at(a0, b0, turn(c0, dc, C))))
                    k += 1
            return full, low, high

        def outer(da, h):
            return piece(me, h, 2 * (da - 1) + h, at(turn(a0, da, A), b0, c0))

        own = outs(0)[0]
        for h in (0, 1):
            for copy in own[h][:C - 1] + own[1 - h][C - 1:]:
                copy.start()
        for da in range(1, A):
            for h in (0, 1):
                outer(da, h).start()

        def step(t, carry):
            @pl.when(jnp.logical_and(t >= 1, t < A))
            def _():
                src = at(turn(a0, t, A), b0, c0)
                full = outs(t)[0]
                for h in (0, 1):
                    piece(src, h, 0, src).wait_recv()
                    for copy in full[h]:
                        copy.start()

            @pl.when(jnp.logical_and(t >= 1, t < A + 1))
            def _():
                a = turn(a0, t - 1, A)
                _, low, high = outs(t - 1)
                for i in range(C - 1):
                    c = turn(c0, i + 1, C)
                    piece(at(a, b0, c), 0, 0, at(a0, b0, c)).wait_recv()
                    for copy in low[i * (B - 1):(i + 1) * (B - 1)]:
                        copy.start()
                for i in range(B - 1):
                    b = turn(b0, i + 1, B)
                    piece(at(a, b, c0), 1, 0, at(a0, b, c0)).wait_recv()
                    for copy in high[i * (C - 1):(i + 1) * (C - 1)]:
                        copy.start()

                @pl.when(t == 1)
                def _():
                    before()

                process(at(a, b0, c0))

            @pl.when(t == A + 1)
            def _():
                late()

            @pl.when(t >= 2)
            def _():
                a = turn(a0, t - 2, A)
                for dc in range(1, C):
                    c = turn(c0, dc, C)
                    piece(at(a, b0, c), 1, 0, at(a0, b0, c)).wait_recv()
                    process(at(a, b0, c))
                for db in range(1, B):
                    b = turn(b0, db, B)
                    piece(at(a, b, c0), 0, 0, at(a0, b, c0)).wait_recv()
                    process(at(a, b, c0))
                for db in range(1, B):
                    for dc in range(1, C):
                        b, c = turn(b0, db, B), turn(c0, dc, C)
                        piece(at(a, b, c), 0, 0, at(a0, b, c0)).wait_recv()
                        piece(at(a, b, c), 1, 0, at(a0, b0, c)).wait_recv()
                        process(at(a, b, c))

            return carry

        lax.fori_loop(0, A + 2, step, 0)

        for da in range(1, A):
            for h in (0, 1):
                outer(da, h).wait_send()

        def done(da, carry):
            full, low, high = outs(da)
            for copy in full[0] + full[1] + low + high:
                copy.wait_send()
            return carry

        lax.fori_loop(0, A, done, 0)

    stat_send(0, st_sq)

    def prepare():
        square = to_column(stat_sum(0, st_sq), 128)
        inv_ref[...] = 1.0 / jnp.sqrt(square / width + 1e-05)

    def up(blk):
        x = unpack(xg[blk].astype(F32), rp, dl)
        normed = (x * inv_ref[:, 0:1] * gain3[blk]).astype(BF16)
        acc[...] += lax.dot_general(normed, wt3[blk], NT, preferred_element_type=F32)

    def table():
        loads[2].wait()
        for b in range(n):
            emb3[b] = emb_v[:, b * dl:(b + 1) * dl]

    gather(xg, x_send, x_recv, prepare, up, table)

    gate_pre = acc[0:rows, 0:fl]
    up_proj = acc[0:rows, fl:2 * fl]
    hid = hid_in[...].astype(F32)
    s = jax.nn.sigmoid(gate_pre)
    gate_grad = (hid * up_proj * s * (1.0 + gate_pre * (1.0 - s))).astype(BF16)
    up_grad = (hid * gate_pre * s).astype(BF16)
    hcat[...] = jnp.zeros_like(hcat)
    hcat[0:rows, 0:fl] = gate_grad
    hcat[0:rows, fl:2 * fl] = up_grad
    st_in[1] = to_row(hcat[...].astype(F32) * acc[...])
    stat_send(1, st_pr)

    def product(blk):
        return pack(jnp.dot(hcat[...], wt3[blk], preferred_element_type=F32))

    lo, hi = pl.ds(0, half), pl.ds(half, half)

    def first(a):
        copies = []
        for db in range(1, B):
            for dc in range(1, C):
                b, c = turn(b0, db, B), turn(c0, dc, C)
                blk = at(a, b, c)
                copies.append((blk, remote(part.at[blk, lo], r1y.at[a, c, b0],
                                           s1y.at[blk], q1y.at[a, c, b0], at(a0, b, c0))))
                copies.append((blk, remote(part.at[blk, hi], r1x.at[a, b, c0],
                                           s1x.at[blk], q1x.at[a, b, c0], at(a0, b0, c))))
        return copies

    def second(a):
        copies = []
        for dc in range(1, C):
            c = turn(c0, dc, C)
            blk = at(a, b0, c)
            pair = [remote(part.at[blk, span], r2x.at[a, c0, span], s2.at[blk, h],
                           q2x.at[a, c0, h], at(a0, b0, c)) for h, span in ((1, hi), (0, lo))]
            copies.append((blk, c, 0, pair))
        for db in range(1, B):
            b = turn(b0, db, B)
            blk = at(a, b, c0)
            pair = [remote(part.at[blk, span], r2y.at[a, b0, span], s2.at[blk, h],
                           q2y.at[a, b0, h], at(a0, b, c0)) for h, span in ((0, lo), (1, hi))]
            copies.append((blk, b, 1, pair))
        return copies

    def third(a, h):
        blk = at(a, b0, c0)
        span = (lo, hi)[h]
        return remote(part.at[blk, span], r3.at[a0, span], s3.at[a, h], q3.at[a0, h], at(a, b0, c0))

    def reduce_step(t, carry):
        @pl.when(t < A)
        def _():
            a = turn(a0, lax.rem(t + 1, A), A)
            for i, (blk, copy) in enumerate(first(a)):
                if i % 2 == 0:
                    part[blk] = product(blk).astype(BF16)
                copy.start()
            for i, (blk, _, way, pair) in enumerate(second(a)):
                value = product(blk)
                if way == 0:
                    part[blk, half:] = value[half:].astype(BF16)
                    kept[lax.rem(t, 2), i] = value[:half]
                else:
                    part[blk, :half] = value[:half].astype(BF16)
                    kept[lax.rem(t, 2), i] = value[half:]
                pair[0].start()

        @pl.when(jnp.logical_and(t >= 1, t < A + 1))
        def _():
            a = turn(a0, lax.rem(t, A), A)
            for i, (blk, other, way, pair) in enumerate(second(a)):
                edge = kept[lax.rem(t - 1, 2), i]
                if way == 0:
                    for db in range(1, B):
                        b = turn(b0, db, B)
                        slot = r1y.at[a, other, b]
                        remote(slot, slot, s1y.at[blk], q1y.at[a, other, b], at(a0, b, c0)).wait_recv()
                        edge = edge + r1y[a, other, b].astype(F32)
                    part[blk, :half] = edge.astype(BF16)
                else:
                    for dc in range(1, C):
                        c = turn(c0, dc, C)
                        slot = r1x.at[a, other, c]
                        remote(slot, slot, s1x.at[blk], q1x.at[a, other, c], at(a0, b0, c)).wait_recv()
                        edge = edge + r1x[a, other, c].astype(F32)
                    part[blk, half:] = edge.astype(BF16)
                pair[1].start()

        @pl.when(t >= 2)
        def _():
            a = turn(a0, t - 1, A) if A & (A - 1) else turn(a0, lax.rem(t - 1, A), A)
            blk = at(a, b0, c0)
            sums[...] = product(blk)
            for h, span in ((0, lo), (1, hi)):
                value = sums[span]
                for dc in range(1, C):
                    c = turn(c0, dc, C)
                    slot = r2x.at[a, c, span]
                    remote(slot, slot, s2.at[blk, h], q2x.at[a, c, h], at(a0, b0, c)).wait_recv()
                    value = value + r2x[a, c, span].astype(F32)
                for db in range(1, B):
                    b = turn(b0, db, B)
                    slot = r2y.at[a, b, span]
                    remote(slot, slot, s2.at[blk, h], q2y.at[a, b, h], at(a0, b, c0)).wait_recv()
                    value = value + r2y[a, b, span].astype(F32)
                sums[span] = value

                @pl.when(t < A + 1)
                def _():
                    part[blk, span] = value.astype(BF16)
                    third(a, h).start()

        return carry

    lax.fori_loop(0, A + 2, reduce_step, 0)

    proj = to_column(stat_sum(1, st_pr), 128)
    share = sums[...]
    for da in range(1, A):
        a = turn(a0, da, A)
        for h, span in ((0, lo), (1, hi)):
            slot = r3.at[a, span]
            remote(slot, slot, s3.at[a, h], q3.at[a, h], at(a, b0, c0)).wait_recv()
        share = share + r3[a].astype(F32)
    inv = inv_ref[:, 0:1]
    scaled = unpack(share, rp, dl) * gain3[me]
    cot = jnp.concatenate([cot_in[...].astype(F32), pad], axis=0)
    grad = cot + inv * scaled - x_own * (inv * inv * (proj[:, 0:1] / width))
    gg[me] = pack(grad).astype(BF16)

    def settle(d, carry):
        a = turn(a0, d, A)
        for _, copy in first(a):
            copy.wait_send()
        for _, _, _, pair in second(a):
            for copy in pair:
                copy.wait_send()

        @pl.when(d >= 1)
        def _():
            third(a, 0).wait_send()
            third(a, 1).wait_send()

        return carry

    def score(blk):
        scores[...] += lax.dot_general(unpack(gg[blk], rp, dl), emb3[blk], NT, preferred_element_type=F32)

    gather(gg, g_send, g_recv, lambda: None, score, lambda: None)
    lax.fori_loop(0, A, settle, 0)

    def member_copy(d):
        return remote(scores, others.at[mine], m_send.at[d], m_recv.at[mine],
                      turn(mine, d, members), "member")

    for d in range(1, members):
        member_copy(d).start()
    ids = to_column(ids_in[...].astype(F32), vl)
    entry = (lax.broadcasted_iota(jnp.int32, (rows, vl), 1) + me * vl).astype(F32)
    total = scores[...]
    for d in range(1, members):
        src = turn(mine, d, members)
        remote(others.at[src], others.at[src], m_send.at[d], m_recv.at[src], src, "member").wait_recv()
        total = total + others[src]
    own = jnp.where(ids == entry, total[0:rows], 0.0)
    st_in[2] = to_row(jnp.concatenate([own, jnp.zeros((rp - rows, vl), F32)], axis=0))
    stat_send(2, st_cu)
    current = to_column(stat_sum(2, st_cu), 128)
    out_ref[...] = total[0:rows] - current[0:rows, 0:1]
    for d in range(1, members):
        member_copy(d).wait_send()


def on_device(n, members, layer_input, norm_gain, w_gate, w_up, hidden_cot, output_cot, embed, suffix_ids):
    _, rows, dl = layer_input.shape
    width = norm_gain.shape[1]
    fl = w_gate.shape[2]
    vl = embed.shape[1]
    lines = A, B, C = grid_of(n)
    rp = -(-rows // 32) * 32
    q, r = divmod(dl, 128)
    length = q * rp + (0 if r == 0 else rp // 2 if r <= 64 else rp)
    half = length // 2
    per = 2 * (B - 1) + 2 * (C - 1) + 2 * (B - 1) * (C - 1)
    moves = 2 * (A - 1) + A * per
    vmem = pl.BlockSpec(memory_space=pltpu.VMEM)
    hbm = pl.BlockSpec(memory_space=pl.ANY)
    dma = pltpu.SemaphoreType.DMA
    V = pltpu.VMEM
    scratch = [
        V((n, length, 128), BF16), V((n, length, 128), BF16), V((n, length, 128), BF16),
        V((A, C, B, half, 128), BF16), V((A, B, C, half, 128), BF16),
        V((A, C, length, 128), BF16), V((A, B, length, 128), BF16), V((A, length, 128), BF16),
        V((3, 1, rp), F32), V((n, 1, rp), F32), V((n, 1, rp), F32), V((n, 1, rp), F32),
        V((fl, width), BF16), V((fl, width), BF16), V((n, 2 * fl, dl), BF16),
        V((vl, width), BF16), V((n, vl, dl), BF16), V((n, 1, dl), F32),
        V((rp, 2 * fl), BF16), V((rp, 2 * fl), F32), V((rp, 128), F32), V((length, 128), F32),
        V((2, B + C - 2, half, 128), F32),
        V((rp, vl), F32), V((members, rp, vl), F32),
        dma((3,)), dma((3, n)), dma((3, n)), dma((moves,)), dma((n, 2)), dma((moves,)), dma((n, 2)),
        dma((n,)), dma((A, C, B)), dma((n,)), dma((A, B, C)), dma((n, 2)), dma((A, C, 2)), dma((A, B, 2)),
        dma((A, 2)), dma((A, 2)), dma((members,)), dma((members,)),
    ]
    return pl.pallas_call(
        functools.partial(kernel, n, members, lines, rows, width),
        out_shape=jax.ShapeDtypeStruct((rows, vl), F32),
        in_specs=[vmem] * 5 + [hbm] * 3,
        out_specs=vmem,
        scratch_shapes=scratch,
        compiler_params=pltpu.CompilerParams(
            collective_id=0, has_side_effects=True, vmem_limit_bytes=56 * 1024 * 1024
        ),
    )(layer_input[0], norm_gain, hidden_cot[0], output_cot[0], suffix_ids[None, :],
      w_gate[0].T, w_up[0].T, embed[0])


def solution(mesh):
    n, members = mesh.shape["shard"], mesh.shape["member"]
    placed = (
        P("member", None, "shard"),
        P("member", None),
        P("member", None, "shard"),
        P("member", None, "shard"),
        P("member", None, "shard"),
        P("member", None, "shard"),
        P("member", "shard", None),
        P(),
    )
    return jax.shard_map(
        functools.partial(on_device, n, members),
        mesh=mesh, in_specs=placed, out_specs=P(None, "shard"), check_vma=False,
    )
```
